32 devices in a mesh: dom: 16 (over z, y, core), region: 2 (over x).
Axes of the slice: x: 2, y: 2, z: 4, core: 2. Of those that a mesh axis runs over, the one named last changes fastest.
Arguments:
- state: float32 [56, 9, 4096], P(None, None, ('dom', 'region')), may hold values from -6 to 6
- stiffness: float32 [3, 56, 56], replicated, may hold values from -0.5 to 0.5
- volume_matrix: float32 [3, 56, 56], replicated, may hold values from -0.5 to 0.5
- trace_matrix: float32 [4, 21, 56], replicated, may hold values from -0.75 to 0.75
- lift_matrix: float32 [4, 56, 21], replicated, may hold values from -0.625 to 0.625
- rotation: float32 [3, 21, 21], replicated, may hold values from -1.25 to 1.25
- star_matrix: float32 [3, 9, 9, 4096], P(None, None, None, ('dom', 'region')), may hold values from -2 to 2
- flux_minus: float32 [4, 9, 9, 4096], P(None, None, None, ('dom', 'region')), may hold values from -2 to 2
- flux_plus: float32 [4, 9, 9, 4096], P(None, None, None, ('dom', 'region')), may hold values from -2 to 2
- patch_rate: int32 [32], P(('dom', 'region')), may hold values from 1 to 4, as said below
- face_orient: int32 [4, 4096], P(None, ('dom', 'region')), may hold values from 0 to 2
- face_source: int32 [4, 4096], P(None, ('dom', 'region')), may hold values from 0 to 703, as said below
- boundary_face: int32 [6, 1024], P(None, ('dom', 'region')), may hold values from 0 to 511, as said below
Outputs:
- final_state: float32 [56, 9, 4096], P(None, None, ('dom', 'region'))
The draws below stay inside these ranges and needn't reach their ends.
Inputs may be any that keep to these rules, and one draw needn't show every extreme that they name: `patch_rate`: every rate is 1, 2 or 4; some patch has rate 4 and some rate 1. `face_source`: a column of the partition's pool: below 512 a local face, else 4 * 128 + 32 k + s; the face boundary_face[k, 32 b + s] of partition b reads exactly column 4 * 128 + 32 k + s, and every other face reads a local face that reads it back. `boundary_face`: local face numbers of the partition; the 192 entries of one partition are distinct.
All inputs are finite; a program needn't handle non-finite values.
Results may differ from the reference program's by a relative error of at most 0.0003.
Values sent between devices are 32-bit elements; how exact they have to be, the bound alone decides.
A program may use at most 64 MiB of HBM per device.

```python
import math
import jax
import jax.numpy as jnp
from jax import lax

NB = 56
NQ = 9
NF = 21
TERMS = 6
TICKS = 4
PATCH = 128
E_DEV = 128
SLOT = 32
ELEMS = 4096
PATCHES = 32
N_DOM = 16
N_REGION = 2


def face_tables(key):
    base = jax.random.fold_in(key, 1234)
    blocks = ELEMS // E_DEV
    faces_all = 4 * E_DEV
    remote_count = 6 * SLOT
    block_keys = jax.random.split(base, blocks)

    def one_block(block_key):
        ordering = jax.random.permutation(block_key, faces_all).astype(jnp.int32)
        places = jnp.arange(faces_all, dtype=jnp.int32)
        partner_place = remote_count + jnp.bitwise_xor(jnp.maximum(places - remote_count, 0), 1)
        partner_face = ordering[jnp.minimum(partner_place, faces_all - 1)]
        values = jnp.where(places < remote_count, faces_all + places, partner_face)
        source_table = jnp.zeros((faces_all,), jnp.int32).at[ordering].set(values)
        return (source_table.reshape(4, E_DEV), ordering[:remote_count].reshape(6, SLOT))
    sources, bounds = jax.vmap(one_block)(block_keys)
    source_table = jnp.transpose(sources, (1, 0, 2)).reshape(4, ELEMS)
    bound_table = jnp.transpose(bounds, (1, 0, 2)).reshape(6, blocks * SLOT)
    return (source_table.astype(jnp.int32), bound_table.astype(jnp.int32))


def draw_face_source(key, part):
    return face_tables(key)[0]


def draw_boundary_face(key, part):
    return face_tables(key)[1]


def draw_patch_rate(key, part):
    base = jax.random.fold_in(key, 77)
    level_key, fast_key = jax.random.split(base, 2)
    levels = jax.random.randint(level_key, (PATCHES,), 0, 3).astype(jnp.int32)
    rates = jnp.left_shift(jnp.ones((PATCHES,), jnp.int32), levels)
    places = jnp.arange(PATCHES, dtype=jnp.int32)
    fast_place = jax.random.randint(fast_key, (), 0, PATCHES).astype(jnp.int32)
    rates = jnp.where(places == fast_place, 4, rates)
    rates = jnp.where(places == (fast_place + 1) % PATCHES, 1, rates)
    return rates.astype(jnp.int32)


def touch_ends(entries, own_key, low, high):
    extent = entries.shape
    place = [jax.random.randint(jax.random.fold_in(own_key, axis), (), 0, extent[axis]) for axis in range(len(extent))]
    entries = entries.at[tuple(place)].set(low)
    longest = extent.index(max(extent))
    place[longest] = (place[longest] + 1) % extent[longest]
    return entries.at[tuple(place)].set(high)


def level_of(rng, shape, shards, least, high):
    def one(dim, blocks):
        steps = jax.random.uniform(jax.random.fold_in(jax.random.fold_in(rng, 6), dim), (blocks,), jnp.float32, least / len(shards), high / len(shards))
        return jnp.repeat(jnp.exp(steps), shape[dim] // blocks).reshape((-1,) + (1,) * (len(shape) - dim - 1))

    level = one(*shards[0])
    for cut in shards[1:]:
        level = level * one(*cut)
    return level


def scatter_about(key, dims, scale, bound, cuts=(), kind=jnp.bfloat16):
    entries = scale * jax.random.normal(key, dims, jnp.float32)
    if cuts:
        entries = entries * level_of(key, dims, cuts, -0.22, 0.18)
    return jnp.clip(entries, -bound, bound).astype(kind)


def setup_inputs(seed: int = 0) -> dict:
    splits = jax.random.split(jax.random.key(seed), 14)
    return {
        "state": scatter_about(splits[0], (NB, NQ, ELEMS), 1.0, 6.0, ((2, 32),), jnp.float32),
        "stiffness": scatter_about(splits[1], (3, NB, NB), (3 * NB) ** -0.5, 0.5, (), jnp.float32),
        "volume_matrix": scatter_about(splits[2], (3, NB, NB), (3 * NB) ** -0.5, 0.5, (), jnp.float32),
        "trace_matrix": scatter_about(splits[3], (4, NF, NB), NB ** -0.5, 0.75, (), jnp.float32),
        "lift_matrix": scatter_about(splits[4], (4, NB, NF), (4 * NF) ** -0.5, 0.625, (), jnp.float32),
        "rotation": scatter_about(splits[5], (3, NF, NF), NF ** -0.5, 1.25, (), jnp.float32),
        "star_matrix": scatter_about(splits[6], (3, NQ, NQ, ELEMS), NQ ** -0.5, 2.0, ((3, 32),), jnp.float32),
        "flux_minus": scatter_about(splits[7], (4, NQ, NQ, ELEMS), NQ ** -0.5, 2.0, ((3, 32),), jnp.float32),
        "flux_plus": scatter_about(splits[8], (4, NQ, NQ, ELEMS), NQ ** -0.5, 2.0, ((3, 32),), jnp.float32),
        "patch_rate": draw_patch_rate(jax.random.fold_in(splits[13], 71), 0),
        "face_orient": touch_ends(jax.random.randint(splits[10], (4, ELEMS), 0, 3), jax.random.fold_in(splits[10], 1), 0, 2).astype(jnp.int32),
        "face_source": draw_face_source(jax.random.fold_in(splits[13], 71), 0),
        "boundary_face": draw_boundary_face(jax.random.fold_in(splits[13], 71), 0),
    }


step_length = 1.5
highest = lax.Precision.HIGHEST


def spatial(matrix, star_matrix, field):
    node_count = matrix.shape[1]
    quantities = field.shape[1]
    elements = field.shape[2]
    unrolled = jnp.transpose(matrix, (1, 0, 2)).reshape(node_count, 3 * node_count)
    starred = jnp.einsum("dpqe,mqe->dmpe", star_matrix, field, precision=highest)
    product = jnp.dot(unrolled, starred.reshape(3 * node_count, quantities * elements), precision=highest, preferred_element_type=jnp.float32)
    return product.reshape(node_count, quantities, elements)


def coefficients(span_ticks, tick_number):
    offset = tick_number % span_ticks
    tick_width = step_length / TICKS
    lower_end = offset.astype(jnp.float32) * tick_width
    upper_end = lower_end + tick_width
    step_width = span_ticks.astype(jnp.float32) * tick_width
    tick_terms = []
    step_terms = []
    for degree in range(TERMS):
        factor = 1.0 / math.factorial(degree + 1)
        tick_terms.append((upper_end ** (degree + 1) - lower_end ** (degree + 1)) * factor)
        step_terms.append(step_width ** (degree + 1) * factor)
    return tick_terms, step_terms, offset == 0, offset == span_ticks - 1


def taylor_terms(field, star_matrix, stiffness):
    derived = [field]
    for degree in range(1, TERMS):
        derived.append(-spatial(stiffness, star_matrix, derived[-1]))
    return jnp.stack(derived)


def combine(derivs, tick_terms, step_terms):
    tick_part = tick_terms[0][None, None, :] * derivs[0]
    step_part = step_terms[0][None, None, :] * derivs[0]
    for degree in range(1, TERMS):
        tick_part = tick_part + tick_terms[degree][None, None, :] * derivs[degree]
        step_part = step_part + step_terms[degree][None, None, :] * derivs[degree]
    return tick_part, step_part


def face_traces(trace_matrix, field):
    node_count = field.shape[0]
    quantities = field.shape[1]
    elements = field.shape[2]
    product = jnp.dot(trace_matrix.reshape(4 * NF, node_count), field.reshape(node_count, quantities * elements), precision=highest, preferred_element_type=jnp.float32)
    return product.reshape(4, NF, quantities, elements)


def local_pool(traces):
    elements = traces.shape[3]
    return jnp.transpose(traces, (1, 2, 0, 3)).reshape(NF * NQ, 4 * elements)


def outgoing(pool_local, boundary_face):
    slots = boundary_face.shape[1]
    picked = jnp.take(pool_local, boundary_face.reshape(-1), axis=1)
    return jnp.transpose(picked.reshape(NF * NQ, 6, slots), (1, 0, 2))


def incoming(pool_local, received, face_source):
    elements = face_source.shape[1]
    extra = jnp.transpose(received, (1, 0, 2)).reshape(NF * NQ, -1)
    whole_pool = jnp.concatenate([pool_local, extra], axis=1)
    picked = jnp.take(whole_pool, face_source.reshape(-1), axis=1)
    return jnp.transpose(picked.reshape(NF, NQ, 4, elements), (2, 0, 1, 3))


def update(current, step_part, accum, star_matrix, flux_minus, flux_plus, face_orient, volume_matrix, trace_matrix, lift_matrix, rotation, finish):
    node_count = current.shape[0]
    quantities = current.shape[1]
    elements = current.shape[2]
    own_trace = face_traces(trace_matrix, step_part)
    chooser = (face_orient[None, :, :] == jnp.arange(3, dtype=jnp.int32)[:, None, None]).astype(jnp.float32)
    turned = jnp.einsum("ojk,fkqe,ofe->fjqe", rotation, accum, chooser, precision=highest)
    flux = jnp.einsum("fpqe,fjqe->fjpe", flux_minus, own_trace, precision=highest) + jnp.einsum("fpqe,fjqe->fjpe", flux_plus, turned, precision=highest)
    lifting = jnp.transpose(lift_matrix, (1, 0, 2)).reshape(node_count, 4 * NF)
    lifted = jnp.dot(lifting, flux.reshape(4 * NF, quantities * elements), precision=highest, preferred_element_type=jnp.float32).reshape(node_count, quantities, elements)
    change = spatial(volume_matrix, star_matrix, step_part) - lifted
    new_state = jnp.where(finish[None, None, :], current + change, current)
    new_accum = jnp.where(finish[None, None, None, :], jnp.zeros_like(accum), accum)
    return new_state, new_accum


def exchange_boxes(sending):
    blocks = sending.shape[0]
    slots = sending.shape[3]
    grid = sending.reshape(N_DOM, N_REGION, 6, NF * NQ, slots)

    def moved(box_number, axis_number, offset):
        values = grid[:, :, box_number]
        length = values.shape[axis_number]
        places = jnp.arange(length) - offset
        valid = (places >= 0) & (places < length)
        if axis_number == 0:
            valid = valid[:, None, None, None]
        else:
            valid = valid[None, :, None, None]
        return jnp.where(valid, jnp.roll(values, offset, axis_number), jnp.zeros_like(values))

    arrived = [moved(1, 0, -1), moved(0, 0, 1), moved(3, 0, -2), moved(2, 0, 2), moved(5, 1, -1), moved(4, 1, 1)]
    return jnp.stack(arrived, axis=2).reshape(blocks, 6, NF * NQ, slots)


def reference(state, stiffness, volume_matrix, trace_matrix, lift_matrix, rotation, star_matrix, flux_minus, flux_plus, patch_rate, face_orient, face_source, boundary_face):
    blocks = ELEMS // E_DEV

    def split_blocks(values):
        leading = values.shape[:-1]
        return jnp.moveaxis(values.reshape(leading + (blocks, E_DEV)), -2, 0)

    current = split_blocks(state)
    star_blocks = split_blocks(star_matrix)
    minus_blocks = split_blocks(flux_minus)
    plus_blocks = split_blocks(flux_plus)
    orient_blocks = split_blocks(face_orient)
    source_blocks = split_blocks(face_source)
    bound_blocks = jnp.moveaxis(boundary_face.reshape(6, blocks, SLOT), 1, 0)
    span_blocks = (TICKS // jnp.repeat(patch_rate, PATCH, total_repeat_length=ELEMS)).astype(jnp.int32).reshape(blocks, E_DEV)
    held_start = current
    accum = jnp.zeros((blocks, 4, NF, NQ, E_DEV), jnp.float32)
    for tick_number in range(TICKS):
        def first_half(items):
            state_block, start_block, star_block, span_block, bound_block = items
            tick_terms, step_terms, starting, finish = coefficients(span_block, tick_number)
            start_block = jnp.where(starting[None, None, :], state_block, start_block)
            derivs = taylor_terms(start_block, star_block, stiffness)
            tick_part, step_part = combine(derivs, tick_terms, step_terms)
            pool_block = local_pool(face_traces(trace_matrix, tick_part))
            return start_block, step_part, pool_block, outgoing(pool_block, bound_block)

        held_start, step_parts, pools, sending = lax.map(first_half, (current, held_start, star_blocks, span_blocks, bound_blocks))
        received = exchange_boxes(sending)

        def second_half(items):
            state_block, step_part, pool_block, recv_block, source_block, orient_block, star_block, minus_block, plus_block, accum_block, span_block = items
            tick_terms, step_terms, starting, finish = coefficients(span_block, tick_number)
            accum_block = accum_block + incoming(pool_block, recv_block, source_block)
            return update(state_block, step_part, accum_block, star_block, minus_block, plus_block, orient_block, volume_matrix, trace_matrix, lift_matrix, rotation, finish)

        current, accum = lax.map(second_half, (current, step_parts, pools, received, source_blocks, orient_blocks, star_blocks, minus_blocks, plus_blocks, accum, span_blocks))
    return jnp.moveaxis(current, 0, -2).reshape(NB, NQ, ELEMS)
```

```python
import functools
import math

import jax
import jax.numpy as jnp
from jax import lax
from jax.experimental import pallas as pl
from jax.experimental.pallas import tpu as pltpu
from jax.sharding import PartitionSpec as P

MESH = pl.DeviceIdType.MESH
TERMS = 6
TICKS = 4
PATCH = 128
STEP_LENGTH = 1.5
f32 = jnp.float32
bf16 = jnp.bfloat16

MOVES = (("dom", 1), ("dom", -1), ("dom", 2), ("dom", -2), ("region", 1), ("region", -1))


def up(n, m):
    return -(-n // m) * m


def high_part(x):
    return x.astype(bf16).astype(f32)


def dot(a, b):
    return jnp.dot(a, b, preferred_element_type=f32)


def kernel(
    sizes,
    rate_ref, state_ref, stiff_ref, vol_ref, trace_ref, lift_ref, rot_ref,
    star_ref, minus_ref, plus_ref, orient_ref, source_ref, bound_ref,
    out_ref,
    coef, wk, wv, wt, wl, wr, tmp, pick_in, pick_out,
    xs, y, itick, istep, volume, pool, acc, own, flux, send_buf, recv_buf,
    send_sem, recv_sem,
):
    nb, nq, nf, e, slots = sizes
    kp = up(nb, 16)
    jp = up(nf, 8)
    rows = nq * jp
    prow = pool.shape[0]
    nface = 4 * e
    nbox = 6 * slots
    place = {"dom": lax.axis_index("dom"), "region": lax.axis_index("region")}
    extent = {"dom": lax.axis_size("dom"), "region": lax.axis_size("region")}
    there = []
    for axis, offset in MOVES:
        target = place[axis] + offset
        there.append((target >= 0) & (target < extent[axis]))

    recv_buf[...] = jnp.zeros_like(recv_buf)

    barrier = pltpu.get_barrier_semaphore()
    count = jnp.int32(0)
    for (axis, offset), ok in zip(MOVES, there):
        @pl.when(ok)
        def _():
            pl.semaphore_signal(barrier, inc=1, device_id={axis: place[axis] + offset}, device_id_type=MESH)
        count = count + ok.astype(jnp.int32)

    def left(dst, blocks, stride, width):
        tmp[...] = jnp.zeros_like(tmp)
        for row, lane, value in blocks:
            hi = high_part(value)
            lo = value - hi
            r, c = value.shape
            for i, part in enumerate((hi, hi, lo)):
                tmp[row:row + r, i * stride + lane:i * stride + lane + c] = part
        dst[...] = tmp[0:dst.shape[0], 0:dst.shape[1]].astype(bf16)

    left(wk, [(d * nb, 0, -stiff_ref[d]) for d in range(3)], kp, nb)
    left(wv, [(d * nb, 0, vol_ref[d]) for d in range(3)], kp, nb)
    left(wt, [(f * jp, 0, trace_ref[f]) for f in range(4)], kp, nb)
    left(wl, [(0, f * jp, -lift_ref[f]) for f in range(4)], 4 * jp, nf)
    left(wr, [(o * jp, 0, rot_ref[o]) for o in range(3)], jp, nf)

    for f in range(4):
        want = source_ref[f:f + 1, :]
        ids = lax.broadcasted_iota(jnp.int32, (pick_in.shape[0], e), 0)
        pick_in[:, f * e:(f + 1) * e] = (ids == want).astype(f32).astype(bf16)
    ids = lax.broadcasted_iota(jnp.int32, (nface, slots), 0)
    tmp[...] = jnp.zeros_like(tmp)
    for k in range(6):
        tmp[0:nface, k * slots:(k + 1) * slots] = (ids == bound_ref[k:k + 1, :]).astype(f32)
    pick_out[...] = tmp[0:nface, 0:pick_out.shape[1]].astype(bf16)

    xs[...] = jnp.zeros_like(xs)
    pool[...] = jnp.zeros_like(pool)
    acc[...] = jnp.zeros_like(acc)
    for q in range(nq):
        out_ref[q] = state_ref[q]

    rate = rate_ref[0]
    span = jnp.where(rate == 1, 4, jnp.where(rate == 2, 2, 1))
    width = STEP_LENGTH / TICKS
    step_width = span.astype(f32) * width

    pl.semaphore_wait(barrier, count)

    def cols(q):
        return slice(q * e, (q + 1) * e)

    def put(q, value):
        pad = jnp.zeros((kp - nb, e), f32)
        hi = high_part(value)
        lo = value - hi
        hib = jnp.concatenate([hi, pad], axis=0).astype(bf16)
        xs[0:kp, cols(q)] = hib
        xs[kp:2 * kp, cols(q)] = jnp.concatenate([lo, pad], axis=0).astype(bf16)
        xs[2 * kp:3 * kp, cols(q)] = hib

    def product(w, dst):
        dst[...] = dot(w[...], xs[...])

    def starred(group):
        sums = [None] * len(group)
        for d in range(3):
            for q in range(nq):
                term = y[d * nb:(d + 1) * nb, cols(q)]
                for i, p in enumerate(group):
                    part = star_ref[d, p, q:q + 1, :] * term
                    sums[i] = part if sums[i] is None else sums[i] + part
        return sums

    groups = [list(range(i, min(i + 3, nq))) for i in range(0, nq, 3)]

    def tick(t, carry):
        offset = lax.bitwise_and(t, span - 1)
        lower = offset.astype(f32) * width
        upper = lower + width
        lo_pow, up_pow, st_pow = lower, upper, step_width
        for k in range(TERMS):
            factor = 1.0 / math.factorial(k + 1)
            coef[0, k] = (up_pow - lo_pow) * factor
            coef[1, k] = st_pow * factor
            lo_pow, up_pow, st_pow = lo_pow * lower, up_pow * upper, st_pow * step_width
        keep = jnp.where(offset == 0, 0.0, 1.0).astype(f32)
        finish = jnp.where(offset == span - 1, 1.0, 0.0).astype(f32)

        for q in range(nq):
            value = out_ref[q]
            itick[q] = coef[0, 0] * value
            istep[q] = coef[1, 0] * value
            put(q, value)

        def degree(k, c):
            product(wk, y)
            ct = coef[0, k]
            cs = coef[1, k]
            for group in groups:
                for p, value in zip(group, starred(group)):
                    itick[p] = itick[p] + ct * value
                    istep[p] = istep[p] + cs * value
                    put(p, value)
            return c

        lax.fori_loop(1, TERMS, degree, 0)

        for q in range(nq):
            put(q, itick[q])
        traces = dot(wt[...], xs[...])
        for q in range(nq):
            for f in range(4):
                pool[q * jp:(q + 1) * jp, f * e:(f + 1) * e] = traces[f * jp:(f + 1) * jp, cols(q)]
        pooled = pool[...]
        pool_hi = pooled.astype(bf16)
        pool_lo = (pooled - pool_hi.astype(f32)).astype(bf16)
        picked = dot(pool_hi, pick_out[...]) + dot(pool_lo, pick_out[...])
        send_buf[t] = jnp.transpose(picked)[0:nbox]

        def box(k):
            axis, step = MOVES[k]
            return pltpu.make_async_remote_copy(
                src_ref=send_buf.at[t, pl.ds(k * slots, slots)],
                dst_ref=recv_buf.at[t, pl.ds((k ^ 1) * slots, slots)],
                send_sem=send_sem.at[t, k],
                recv_sem=recv_sem.at[t, k ^ 1],
                device_id={axis: place[axis] + step},
                device_id_type=MESH,
            )

        for k in range(6):
            @pl.when(there[k])
            def _():
                box(k).start()

        local = dot(pool_hi, pick_in[0:nface, :]) + dot(pool_lo, pick_in[0:nface, :])
        acc[...] = acc[...] * keep + local
        for q in range(nq):
            put(q, istep[q])
        own[...] = dot(wt[...], xs[...])
        product(wv, y)
        for group in groups:
            for p, value in zip(group, starred(group)):
                volume[p] = value

        for k in range(6):
            @pl.when(there[k])
            def _():
                axis, step = MOVES[k]
                pltpu.make_async_remote_copy(
                    src_ref=send_buf.at[t, pl.ds(k * slots, slots)],
                    dst_ref=recv_buf.at[t, pl.ds(k * slots, slots)],
                    send_sem=send_sem.at[t, k],
                    recv_sem=recv_sem.at[t, k],
                    device_id={axis: place[axis] + step},
                    device_id_type=MESH,
                ).wait()

        came = jnp.transpose(recv_buf[t])
        came_hi = came.astype(bf16)
        came_lo = (came - came_hi.astype(f32)).astype(bf16)
        remote = pick_in[nface:nface + nbox, :]
        acc[...] = acc[...] + (dot(came_hi, remote) + dot(came_lo, remote))

        spare = jnp.zeros((wr.shape[1] - 3 * jp, nface), f32)
        turned = []
        for q in range(nq):
            value = acc[q * jp:(q + 1) * jp, :]
            hi = high_part(value)
            stack = jnp.concatenate([hi, value - hi, hi, spare], axis=0).astype(bf16)
            y[0:3 * jp, 0:nface] = dot(wr[...], stack)
            for f in range(4):
                orient = orient_ref[f:f + 1, :]
                r0 = y[0:jp, f * e:(f + 1) * e]
                r1 = y[jp:2 * jp, f * e:(f + 1) * e]
                r2 = y[2 * jp:3 * jp, f * e:(f + 1) * e]
                flux[f * jp:(f + 1) * jp, cols(q)] = jnp.where(orient == 0, r0, jnp.where(orient == 1, r1, r2))
        for f in range(4):
            sums = [None] * nq
            for q in range(nq):
                mine = own[f * jp:(f + 1) * jp, cols(q)]
                theirs = flux[f * jp:(f + 1) * jp, cols(q)]
                for p in range(nq):
                    part = minus_ref[f, p, q:q + 1, :] * mine + plus_ref[f, p, q:q + 1, :] * theirs
                    sums[p] = part if sums[p] is None else sums[p] + part
            for p in range(nq):
                own[f * jp:(f + 1) * jp, cols(p)] = sums[p]
        value = own[...]
        hi = high_part(value)
        stack = jnp.concatenate([hi, value - hi, hi], axis=0).astype(bf16)
        y[0:nb, :] = dot(wl[...], stack)
        for p in range(nq):
            now = out_ref[p]
            out_ref[p] = jnp.where(finish > 0.5, now + (volume[p] + y[0:nb, cols(p)]), now)
        return carry

    lax.fori_loop(0, TICKS, tick, 0)


def local(
    state, stiffness, volume_matrix, trace_matrix, lift_matrix, rotation, star_matrix,
    flux_minus, flux_plus, patch_rate, face_orient, face_source, boundary_face,
):
    nb, nq, e = state.shape
    nf = rotation.shape[1]
    slots = boundary_face.shape[1]
    assert patch_rate.shape[0] * PATCH == e and patch_rate.shape[0] == 1
    kp, jp = up(nb, 16), up(nf, 8)
    nface, nbox = 4 * e, 6 * slots
    prow = up(nq * jp, 128)
    vmem = pl.BlockSpec(memory_space=pltpu.VMEM)
    scratch = [
        pltpu.SMEM((2, 8), f32),
        pltpu.VMEM((3 * nb, 3 * kp), bf16),
        pltpu.VMEM((3 * nb, 3 * kp), bf16),
        pltpu.VMEM((4 * jp, 3 * kp), bf16),
        pltpu.VMEM((nb, 12 * jp), bf16),
        pltpu.VMEM((3 * jp, up(3 * jp, 16)), bf16),
        pltpu.VMEM((nface, 3 * 128), f32),
        pltpu.VMEM((nface + nbox, nface), bf16),
        pltpu.VMEM((nface, up(nbox, 128)), bf16),
        pltpu.VMEM((3 * kp, nq * e), bf16),
        pltpu.VMEM((3 * nb, nq * e), f32),
        pltpu.VMEM((nq, nb, e), f32),
        pltpu.VMEM((nq, nb, e), f32),
        pltpu.VMEM((nq, nb, e), f32),
        pltpu.VMEM((prow, nface), f32),
        pltpu.VMEM((prow, nface), f32),
        pltpu.VMEM((4 * jp, nq * e), f32),
        pltpu.VMEM((4 * jp, nq * e), f32),
        pltpu.VMEM((TICKS, nbox, prow), f32),
        pltpu.VMEM((TICKS, nbox, prow), f32),
        pltpu.SemaphoreType.DMA((TICKS, 6)),
        pltpu.SemaphoreType.DMA((TICKS, 6)),
    ]
    out = pl.pallas_call(
        functools.partial(kernel, (nb, nq, nf, e, slots)),
        out_shape=jax.ShapeDtypeStruct((nq, nb, e), f32),
        in_specs=[pl.BlockSpec(memory_space=pltpu.SMEM)] + [vmem] * 12,
        out_specs=vmem,
        scratch_shapes=scratch,
        compiler_params=pltpu.CompilerParams(
            collective_id=0, has_side_effects=True, vmem_limit_bytes=48 * 1024 * 1024
        ),
    )(
        patch_rate, jnp.transpose(state, (1, 0, 2)), stiffness, volume_matrix, trace_matrix,
        lift_matrix, rotation, star_matrix, flux_minus, flux_plus, face_orient, face_source, boundary_face,
    )
    return jnp.transpose(out, (1, 0, 2))


def solution(mesh):
    both = ("dom", "region")
    return jax.shard_map(
        local,
        mesh=mesh,
        in_specs=(
            P(None, None, both), P(), P(), P(), P(), P(),
            P(None, None, None, both), P(None, None, None, both), P(None, None, None, both),
            P(both), P(None, both), P(None, both), P(None, both),
        ),
        out_specs=P(None, None, both),
        check_vma=False,
    )
```

```python
import functools
import math

import jax
import jax.numpy as jnp
from jax import lax
from jax.experimental import pallas as pl
from jax.experimental.pallas import tpu as pltpu
from jax.sharding import PartitionSpec as P

MESH = pl.DeviceIdType.MESH
TERMS = 6
TICKS = 4
PATCH = 128
STEP_LENGTH = 1.5
f32 = jnp.float32
bf16 = jnp.bfloat16

MOVES = (("dom", 1), ("dom", -1), ("dom", 2), ("dom", -2), ("region", 1), ("region", -1))


def up(n, m):
    return -(-n // m) * m


def high_part(x):
    return x.astype(bf16).astype(f32)


def dot(a, b):
    return jnp.dot(a, b, preferred_element_type=f32)


def kernel(
    sizes,
    rate_ref, state_ref, stiff_ref, vol_ref, trace_ref, lift_ref, rot_ref,
    star_ref, minus_ref, plus_ref, orient_ref, source_ref, bound_ref,
    out_ref,
    coef, wk, wv, wt, wl, wr, tmp, pick_in, pick_out,
    xs, y, itick, istep, volume, pool, acc, own, flux, send_buf, recv_buf,
    send_sem, recv_sem,
):
    nb, nq, nf, e, slots = sizes
    kp = up(nb, 16)
    jp = up(nf, 8)
    rows = nq * jp
    prow = send_buf.shape[2]
    mrow = pool.shape[0]
    nface = 4 * e
    nbox = 6 * slots
    place = {"dom": lax.axis_index("dom"), "region": lax.axis_index("region")}
    extent = {"dom": lax.axis_size("dom"), "region": lax.axis_size("region")}
    there = []
    for axis, offset in MOVES:
        target = place[axis] + offset
        there.append((target >= 0) & (target < extent[axis]))

    recv_buf[...] = jnp.zeros_like(recv_buf)

    barrier = pltpu.get_barrier_semaphore()
    count = jnp.int32(0)
    for (axis, offset), ok in zip(MOVES, there):
        @pl.when(ok)
        def _():
            pl.semaphore_signal(barrier, inc=1, device_id={axis: place[axis] + offset}, device_id_type=MESH)
        count = count + ok.astype(jnp.int32)

    def left(dst, blocks, stride, width):
        tmp[...] = jnp.zeros_like(tmp)
        for row, lane, value in blocks:
            hi = high_part(value)
            lo = value - hi
            r, c = value.shape
            for i, part in enumerate((hi, hi, lo)):
                tmp[row:row + r, i * stride + lane:i * stride + lane + c] = part
        dst[...] = tmp[0:dst.shape[0], 0:dst.shape[1]].astype(bf16)

    left(wk, [(d * nb, 0, -stiff_ref[d]) for d in range(3)], kp, nb)
    left(wv, [(d * nb, 0, vol_ref[d]) for d in range(3)]
         + [(3 * nb + f * jp, 0, trace_ref[:, f, :]) for f in range(4)], kp, nb)
    left(wt, [(f * jp, 0, trace_ref[:, f, :]) for f in range(4)], kp, nb)
    left(wl, [(0, f * jp, -jnp.transpose(lift_ref[:, f, :])) for f in range(4)], 4 * jp, nf)
    left(wr, [(o * jp, 0, rot_ref[o]) for o in range(3)], jp, nf)

    for f in range(4):
        want = source_ref[f:f + 1, :]
        ids = lax.broadcasted_iota(jnp.int32, (pick_in.shape[0], e), 0)
        pick_in[:, f * e:(f + 1) * e] = (ids == want).astype(f32).astype(bf16)
    ids = lax.broadcasted_iota(jnp.int32, (nface, slots), 0)
    tmp[...] = jnp.zeros_like(tmp)
    for k in range(6):
        tmp[0:nface, k * slots:(k + 1) * slots] = (ids == bound_ref[k:k + 1, :]).astype(f32)
    pick_out[...] = tmp[0:nface, 0:pick_out.shape[1]].astype(bf16)

    xs[...] = jnp.zeros_like(xs)
    pool[...] = jnp.zeros_like(pool)
    acc[...] = jnp.zeros_like(acc)
    for q in range(nq):
        out_ref[q] = state_ref[q]

    rate = rate_ref[0]
    span = jnp.where(rate == 1, 4, jnp.where(rate == 2, 2, 1))
    width = STEP_LENGTH / TICKS
    step_width = span.astype(f32) * width

    pl.semaphore_wait(barrier, count)

    def cols(q):
        if isinstance(q, int):
            return slice(q * e, (q + 1) * e)
        return pl.ds(pl.multiple_of(q * e, e), e)

    def put(q, value):
        pad = jnp.zeros((kp - nb, e), f32)
        hi = high_part(value)
        lo = value - hi
        hib = jnp.concatenate([hi, pad], axis=0).astype(bf16)
        xs[0:kp, cols(q)] = hib
        xs[kp:2 * kp, cols(q)] = jnp.concatenate([lo, pad], axis=0).astype(bf16)
        xs[2 * kp:3 * kp, cols(q)] = hib

    def starred(group):
        sums = [None] * len(group)
        for d in range(3):
            for q in range(nq):
                term = y[d * nb:(d + 1) * nb, cols(q)]
                for i, p in enumerate(group):
                    part = star_ref[p, q, d:d + 1, :] * term
                    sums[i] = part if sums[i] is None else sums[i] + part
        return sums

    gsize = next(n for n in (3, 2, 1) if nq % n == 0)

    def by_group(use):
        def body(g, c):
            use([g * gsize + i for i in range(gsize)])
            return c

        lax.fori_loop(0, nq // gsize, body, 0)

    def both(value):
        hi = high_part(value)
        return jnp.concatenate([hi, value - hi], axis=0).astype(bf16)

    def gather(value, table):
        n = value.shape[0]
        result = dot(both(value), table)
        return result[0:n] + result[n:2 * n]

    def solver(matrix_ref, group, start, field, base):
        for f in range(4):
            sums = [start(f, p) for p in group]
            for q in range(nq):
                term = field[base + f * jp:base + (f + 1) * jp, cols(q)]
                for i, p in enumerate(group):
                    part = matrix_ref[p, q, f:f + 1, :] * term
                    sums[i] = part if sums[i] is None else sums[i] + part
            for p, value in zip(group, sums):
                own[f * jp:(f + 1) * jp, cols(p)] = value

    def tick(t, carry):
        offset = lax.bitwise_and(t, span - 1)
        lower = offset.astype(f32) * width
        upper = lower + width
        lo_pow, up_pow, st_pow = lower, upper, step_width
        for k in range(TERMS):
            factor = 1.0 / math.factorial(k + 1)
            coef[0, k] = (up_pow - lo_pow) * factor
            coef[1, k] = st_pow * factor
            lo_pow, up_pow, st_pow = lo_pow * lower, up_pow * upper, st_pow * step_width
        keep = jnp.where(offset == 0, 0.0, 1.0).astype(f32)
        finish = jnp.where(offset == span - 1, 1.0, 0.0).astype(f32)

        for q in range(nq):
            value = out_ref[q]
            itick[q] = coef[0, 0] * value
            istep[q] = coef[1, 0] * value
            put(q, value)

        def degree(k, c):
            y[0:3 * nb, :] = dot(wk[...], xs[...])
            ct = coef[0, k]
            cs = coef[1, k]

            def use(group):
                for p, value in zip(group, starred(group)):
                    itick[p] = itick[p] + ct * value
                    istep[p] = istep[p] + cs * value
                    put(p, value)

            by_group(use)
            return c

        lax.fori_loop(1, TERMS, degree, 0)

        for q in range(nq):
            put(q, itick[q])
        traces = dot(wt[...], xs[...])
        for q in range(nq):
            for f in range(4):
                pool[q * jp:(q + 1) * jp, f * e:(f + 1) * e] = traces[f * jp:(f + 1) * jp, cols(q)]
        pooled = pool[0:mrow, :]
        picked = gather(pooled, pick_out[...])
        if prow > mrow:
            picked = jnp.concatenate([picked, jnp.zeros((prow - mrow, picked.shape[1]), f32)], axis=0)
        send_buf[t] = jnp.transpose(picked)[0:nbox]

        def box(k):
            axis, step = MOVES[k]
            return pltpu.make_async_remote_copy(
                src_ref=send_buf.at[t, pl.ds(k * slots, slots)],
                dst_ref=recv_buf.at[t, pl.ds((k ^ 1) * slots, slots)],
                send_sem=send_sem.at[t, k],
                recv_sem=recv_sem.at[t, k ^ 1],
                device_id={axis: place[axis] + step},
                device_id_type=MESH,
            )

        for k in range(6):
            @pl.when(there[k])
            def _():
                box(k).start()

        acc[...] = acc[...] * keep + gather(pooled, pick_in[0:nface, :])
        for q in range(nq):
            put(q, istep[q])
        y[...] = dot(wv[...], xs[...])

        def use(group):
            for p, value in zip(group, starred(group)):
                volume[p] = value
            solver(minus_ref, group, lambda f, p: None, y, 3 * nb)

        by_group(use)

        for k in range(6):
            @pl.when(there[k])
            def _():
                axis, step = MOVES[k]
                pltpu.make_async_remote_copy(
                    src_ref=send_buf.at[t, pl.ds(k * slots, slots)],
                    dst_ref=recv_buf.at[t, pl.ds(k * slots, slots)],
                    send_sem=send_sem.at[t, k],
                    recv_sem=recv_sem.at[t, k],
                    device_id={axis: place[axis] + step},
                    device_id_type=MESH,
                ).wait()

        came = jnp.transpose(recv_buf[t])[0:mrow]
        acc[...] = acc[...] + gather(came, pick_in[nface:nface + nbox, :])

        spare = jnp.zeros((wr.shape[1] - 3 * jp, nface), f32)
        for q in range(nq):
            value = acc[q * jp:(q + 1) * jp, :]
            hi = high_part(value)
            stack = jnp.concatenate([hi, value - hi, hi, spare], axis=0).astype(bf16)
            y[0:3 * jp, 0:nface] = dot(wr[...], stack)
            for f in range(4):
                orient = orient_ref[f:f + 1, :]
                r0 = y[0:jp, f * e:(f + 1) * e]
                r1 = y[jp:2 * jp, f * e:(f + 1) * e]
                r2 = y[2 * jp:3 * jp, f * e:(f + 1) * e]
                flux[f * jp:(f + 1) * jp, cols(q)] = jnp.where(orient == 0, r0, jnp.where(orient == 1, r1, r2))
        by_group(lambda group: solver(plus_ref, group, lambda f, p: own[f * jp:(f + 1) * jp, cols(p)], flux, 0))
        value = own[...]
        hi = high_part(value)
        stack = jnp.concatenate([hi, value - hi, hi], axis=0).astype(bf16)
        y[0:nb, :] = dot(wl[...], stack)
        for p in range(nq):
            now = out_ref[p]
            out_ref[p] = jnp.where(finish > 0.5, now + (volume[p] + y[0:nb, cols(p)]), now)
        return carry

    lax.fori_loop(0, TICKS, tick, 0)


def local(
    state, stiffness, volume_matrix, trace_matrix, lift_matrix, rotation, star_matrix,
    flux_minus, flux_plus, patch_rate, face_orient, face_source, boundary_face,
):
    nb, nq, e = state.shape
    nf = rotation.shape[1]
    slots = boundary_face.shape[1]
    assert patch_rate.shape[0] * PATCH == e and patch_rate.shape[0] == 1
    kp, jp = up(nb, 16), up(nf, 8)
    nface, nbox = 4 * e, 6 * slots
    mrow = up(nq * jp, 16)
    prow = up(mrow, 128)
    vmem = pl.BlockSpec(memory_space=pltpu.VMEM)
    scratch = [
        pltpu.SMEM((2, 8), f32),
        pltpu.VMEM((3 * nb, 3 * kp), bf16),
        pltpu.VMEM((3 * nb + 4 * jp, 3 * kp), bf16),
        pltpu.VMEM((4 * jp, 3 * kp), bf16),
        pltpu.VMEM((nb, 12 * jp), bf16),
        pltpu.VMEM((3 * jp, up(3 * jp, 16)), bf16),
        pltpu.VMEM((nface, 3 * 128), f32),
        pltpu.VMEM((nface + nbox, nface), bf16),
        pltpu.VMEM((nface, up(nbox, 128)), bf16),
        pltpu.VMEM((3 * kp, nq * e), bf16),
        pltpu.VMEM((3 * nb + 4 * jp, nq * e), f32),
        pltpu.VMEM((nq, nb, e), f32),
        pltpu.VMEM((nq, nb, e), f32),
        pltpu.VMEM((nq, nb, e), f32),
        pltpu.VMEM((mrow, nface), f32),
        pltpu.VMEM((mrow, nface), f32),
        pltpu.VMEM((4 * jp, nq * e), f32),
        pltpu.VMEM((4 * jp, nq * e), f32),
        pltpu.VMEM((TICKS, nbox, prow), f32),
        pltpu.VMEM((TICKS, nbox, prow), f32),
        pltpu.SemaphoreType.DMA((TICKS, 6)),
        pltpu.SemaphoreType.DMA((TICKS, 6)),
    ]
    out = pl.pallas_call(
        functools.partial(kernel, (nb, nq, nf, e, slots)),
        out_shape=jax.ShapeDtypeStruct((nq, nb, e), f32),
        in_specs=[pl.BlockSpec(memory_space=pltpu.SMEM)] + [vmem] * 12,
        out_specs=vmem,
        scratch_shapes=scratch,
        compiler_params=pltpu.CompilerParams(
            collective_id=0, has_side_effects=True, vmem_limit_bytes=48 * 1024 * 1024
        ),
    )(
        patch_rate, jnp.transpose(state, (1, 0, 2)), stiffness, volume_matrix,
        jnp.transpose(trace_matrix, (1, 0, 2)), jnp.transpose(lift_matrix, (2, 0, 1)), rotation,
        *(jnp.transpose(m, (1, 2, 0, 3)) for m in (star_matrix, flux_minus, flux_plus)),
        face_orient, face_source, boundary_face,
    )
    return jnp.transpose(out, (1, 0, 2))


def solution(mesh):
    both = ("dom", "region")
    return jax.shard_map(
        local,
        mesh=mesh,
        in_specs=(
            P(None, None, both), P(), P(), P(), P(), P(),
            P(None, None, None, both), P(None, None, None, both), P(None, None, None, both),
            P(both), P(None, both), P(None, both), P(None, both),
        ),
        out_specs=P(None, None, both),
        check_vma=False,
    )
```

```python
import functools
import math

import jax
import jax.numpy as jnp
from jax import lax
from jax.experimental import pallas as pl
from jax.experimental.pallas import tpu as pltpu
from jax.sharding import PartitionSpec as P

MESH = pl.DeviceIdType.MESH
TERMS = 6
TICKS = 4
PATCH = 128
STEP_LENGTH = 1.5
f32 = jnp.float32
bf16 = jnp.bfloat16

MOVES = (("dom", 1), ("dom", -1), ("dom", 2), ("dom", -2), ("region", 1), ("region", -1))


def up(n, m):
    return -(-n // m) * m


def high_part(x):
    return x.astype(bf16).astype(f32)


def dot(a, b):
    return jnp.dot(a, b, preferred_element_type=f32)


def kernel(
    sizes,
    rate_ref, *refs,
):
    sources, out_ref, held = refs[:12], refs[12], refs[13:24]
    (
        coef, load_sem, wk, wv, wt, wl, wr, tmp, pick_in, pick_out,
        xs, y, itick, istep, volume, pool, acc, own, flux, send_buf, recv_buf,
        send_sem, recv_sem,
    ) = refs[24:]
    (
        stiff_ref, vol_ref, trace_ref, lift_ref, rot_ref,
        star_ref, minus_ref, plus_ref, orient_ref, source_ref, bound_ref,
    ) = held
    loads = [
        pltpu.make_async_copy(src, dst, load_sem.at[i])
        for i, (src, dst) in enumerate(zip(sources, (out_ref, *held)))
    ]
    for i in (1, 2, 3, 4, 5, 10, 11, 0, 6, 7, 8, 9):
        loads[i].start()
    nb, nq, nf, e, slots = sizes
    kp = up(nb, 16)
    jp = up(nf, 8)
    rows = nq * jp
    prow = send_buf.shape[2]
    mrow = pool.shape[0]
    nface = 4 * e
    nbox = 6 * slots
    place = {"dom": lax.axis_index("dom"), "region": lax.axis_index("region")}
    extent = {"dom": lax.axis_size("dom"), "region": lax.axis_size("region")}
    there = []
    for axis, offset in MOVES:
        target = place[axis] + offset
        there.append((target >= 0) & (target < extent[axis]))

    recv_buf[...] = jnp.zeros_like(recv_buf)

    barrier = pltpu.get_barrier_semaphore()
    count = jnp.int32(0)
    for (axis, offset), ok in zip(MOVES, there):
        @pl.when(ok)
        def _():
            pl.semaphore_signal(barrier, inc=1, device_id={axis: place[axis] + offset}, device_id_type=MESH)
        count = count + ok.astype(jnp.int32)

    for i in (1, 2, 3, 4, 5):
        loads[i].wait()

    def left(dst, blocks, stride, width):
        tmp[...] = jnp.zeros_like(tmp)
        for row, lane, value in blocks:
            hi = high_part(value)
            lo = value - hi
            r, c = value.shape
            for i, part in enumerate((hi, hi, lo)):
                tmp[row:row + r, i * stride + lane:i * stride + lane + c] = part
        dst[...] = tmp[0:dst.shape[0], 0:dst.shape[1]].astype(bf16)

    left(wk, [(d * nb, 0, -stiff_ref[d]) for d in range(3)], kp, nb)
    left(wv, [(d * nb, 0, vol_ref[d]) for d in range(3)]
         + [(3 * nb + f * jp, 0, trace_ref[:, f, :]) for f in range(4)], kp, nb)
    left(wt, [(f * jp, 0, trace_ref[:, f, :]) for f in range(4)], kp, nb)
    left(wl, [(0, f * jp, -jnp.transpose(lift_ref[:, f, :])) for f in range(4)], 4 * jp, nf)
    left(wr, [(o * jp, 0, rot_ref[o]) for o in range(3)], jp, nf)

    loads[10].wait()
    loads[11].wait()

    for f in range(4):
        want = source_ref[f:f + 1, :]
        ids = lax.broadcasted_iota(jnp.int32, (pick_in.shape[0], e), 0)
        pick_in[:, f * e:(f + 1) * e] = (ids == want).astype(f32).astype(bf16)
    ids = lax.broadcasted_iota(jnp.int32, (nface, slots), 0)
    tmp[...] = jnp.zeros_like(tmp)
    for k in range(6):
        tmp[0:nface, k * slots:(k + 1) * slots] = (ids == bound_ref[k:k + 1, :]).astype(f32)
    pick_out[...] = tmp[0:nface, 0:pick_out.shape[1]].astype(bf16)

    xs[...] = jnp.zeros_like(xs)
    pool[...] = jnp.zeros_like(pool)
    acc[...] = jnp.zeros_like(acc)
    for i in (0, 6, 7, 8, 9):
        loads[i].wait()

    rate = rate_ref[0]
    span = jnp.where(rate == 1, 4, jnp.where(rate == 2, 2, 1))
    width = STEP_LENGTH / TICKS
    step_width = span.astype(f32) * width

    pl.semaphore_wait(barrier, count)

    def cols(q):
        if isinstance(q, int):
            return slice(q * e, (q + 1) * e)
        return pl.ds(pl.multiple_of(q * e, e), e)

    def put(q, value):
        pad = jnp.zeros((kp - nb, e), f32)
        hi = high_part(value)
        lo = value - hi
        hib = jnp.concatenate([hi, pad], axis=0).astype(bf16)
        xs[0:kp, cols(q)] = hib
        xs[kp:2 * kp, cols(q)] = jnp.concatenate([lo, pad], axis=0).astype(bf16)
        xs[2 * kp:3 * kp, cols(q)] = hib

    def starred(group):
        sums = [None] * len(group)
        for d in range(3):
            for q in range(nq):
                term = y[d * nb:(d + 1) * nb, cols(q)]
                for i, p in enumerate(group):
                    part = star_ref[p, q, d:d + 1, :] * term
                    sums[i] = part if sums[i] is None else sums[i] + part
        return sums

    gsize = next(n for n in (3, 2, 1) if nq % n == 0)

    def by_group(use):
        def body(g, c):
            use([g * gsize + i for i in range(gsize)])
            return c

        lax.fori_loop(0, nq // gsize, body, 0)

    def both(value):
        hi = high_part(value)
        return jnp.concatenate([hi, value - hi], axis=0).astype(bf16)

    def gather(value, table):
        n = value.shape[0]
        result = dot(both(value), table)
        return result[0:n] + result[n:2 * n]

    def solver(matrix_ref, group, start, field, base):
        for f in range(4):
            sums = [start(f, p) for p in group]
            for q in range(nq):
                term = field[base + f * jp:base + (f + 1) * jp, cols(q)]
                for i, p in enumerate(group):
                    part = matrix_ref[p, q, f:f + 1, :] * term
                    sums[i] = part if sums[i] is None else sums[i] + part
            for p, value in zip(group, sums):
                own[f * jp:(f + 1) * jp, cols(p)] = value

    def tick(t, carry):
        offset = lax.bitwise_and(t, span - 1)
        lower = offset.astype(f32) * width
        upper = lower + width
        lo_pow, up_pow, st_pow = lower, upper, step_width
        for k in range(TERMS):
            factor = 1.0 / math.factorial(k + 1)
            coef[0, k] = (up_pow - lo_pow) * factor
            coef[1, k] = st_pow * factor
            lo_pow, up_pow, st_pow = lo_pow * lower, up_pow * upper, st_pow * step_width
        keep = jnp.where(offset == 0, 0.0, 1.0).astype(f32)
        finish = jnp.where(offset == span - 1, 1.0, 0.0).astype(f32)

        for q in range(nq):
            value = out_ref[q]
            itick[q] = coef[0, 0] * value
            istep[q] = coef[1, 0] * value
            put(q, value)

        def degree(k, c):
            y[0:3 * nb, :] = dot(wk[...], xs[...])
            ct = coef[0, k]
            cs = coef[1, k]

            def use(group):
                for p, value in zip(group, starred(group)):
                    itick[p] = itick[p] + ct * value
                    istep[p] = istep[p] + cs * value
                    put(p, value)

            by_group(use)
            return c

        lax.fori_loop(1, TERMS, degree, 0)

        for q in range(nq):
            put(q, itick[q])
        traces = dot(wt[...], xs[...])
        for q in range(nq):
            for f in range(4):
                pool[q * jp:(q + 1) * jp, f * e:(f + 1) * e] = traces[f * jp:(f + 1) * jp, cols(q)]
        pooled = pool[0:mrow, :]
        picked = gather(pooled, pick_out[...])
        if prow > mrow:
            picked = jnp.concatenate([picked, jnp.zeros((prow - mrow, picked.shape[1]), f32)], axis=0)
        send_buf[t] = jnp.transpose(picked)[0:nbox]

        def box(k):
            axis, step = MOVES[k]
            return pltpu.make_async_remote_copy(
                src_ref=send_buf.at[t, pl.ds(k * slots, slots)],
                dst_ref=recv_buf.at[t, pl.ds((k ^ 1) * slots, slots)],
                send_sem=send_sem.at[t, k],
                recv_sem=recv_sem.at[t, k ^ 1],
                device_id={axis: place[axis] + step},
                device_id_type=MESH,
            )

        for k in range(6):
            @pl.when(there[k])
            def _():
                box(k).start()

        acc[...] = acc[...] * keep + gather(pooled, pick_in[0:nface, :])
        for q in range(nq):
            put(q, istep[q])
        y[...] = dot(wv[...], xs[...])

        def use(group):
            for p, value in zip(group, starred(group)):
                volume[p] = value
            solver(minus_ref, group, lambda f, p: None, y, 3 * nb)

        by_group(use)

        for k in range(6):
            @pl.when(there[k])
            def _():
                axis, step = MOVES[k]
                pltpu.make_async_remote_copy(
                    src_ref=send_buf.at[t, pl.ds(k * slots, slots)],
                    dst_ref=recv_buf.at[t, pl.ds(k * slots, slots)],
                    send_sem=send_sem.at[t, k],
                    recv_sem=recv_sem.at[t, k],
                    device_id={axis: place[axis] + step},
                    device_id_type=MESH,
                ).wait()

        came = jnp.transpose(recv_buf[t])[0:mrow]
        acc[...] = acc[...] + gather(came, pick_in[nface:nface + nbox, :])

        spare = jnp.zeros((wr.shape[1] - 3 * jp, nface), f32)
        for q in range(nq):
            value = acc[q * jp:(q + 1) * jp, :]
            hi = high_part(value)
            stack = jnp.concatenate([hi, value - hi, hi, spare], axis=0).astype(bf16)
            y[0:3 * jp, 0:nface] = dot(wr[...], stack)
            for f in range(4):
                orient = orient_ref[f:f + 1, :]
                r0 = y[0:jp, f * e:(f + 1) * e]
                r1 = y[jp:2 * jp, f * e:(f + 1) * e]
                r2 = y[2 * jp:3 * jp, f * e:(f + 1) * e]
                flux[f * jp:(f + 1) * jp, cols(q)] = jnp.where(orient == 0, r0, jnp.where(orient == 1, r1, r2))
        by_group(lambda group: solver(plus_ref, group, lambda f, p: own[f * jp:(f + 1) * jp, cols(p)], flux, 0))
        value = own[...]
        hi = high_part(value)
        stack = jnp.concatenate([hi, value - hi, hi], axis=0).astype(bf16)
        y[0:nb, :] = dot(wl[...], stack)
        for p in range(nq):
            now = out_ref[p]
            out_ref[p] = jnp.where(finish > 0.5, now + (volume[p] + y[0:nb, cols(p)]), now)
        return carry

    lax.fori_loop(0, TICKS, tick, 0)


def local(
    state, stiffness, volume_matrix, trace_matrix, lift_matrix, rotation, star_matrix,
    flux_minus, flux_plus, patch_rate, face_orient, face_source, boundary_face,
):
    nb, nq, e = state.shape
    nf = rotation.shape[1]
    slots = boundary_face.shape[1]
    assert patch_rate.shape[0] * PATCH == e and patch_rate.shape[0] == 1
    kp, jp = up(nb, 16), up(nf, 8)
    nface, nbox = 4 * e, 6 * slots
    mrow = up(nq * jp, 16)
    prow = up(mrow, 128)
    vmem = pl.BlockSpec(memory_space=pltpu.VMEM)
    scratch = [
        pltpu.SMEM((2, 8), f32),
        pltpu.SemaphoreType.DMA((12,)),
        pltpu.VMEM((3 * nb, 3 * kp), bf16),
        pltpu.VMEM((3 * nb + 4 * jp, 3 * kp), bf16),
        pltpu.VMEM((4 * jp, 3 * kp), bf16),
        pltpu.VMEM((nb, 12 * jp), bf16),
        pltpu.VMEM((3 * jp, up(3 * jp, 16)), bf16),
        pltpu.VMEM((nface, 3 * 128), f32),
        pltpu.VMEM((nface + nbox, nface), bf16),
        pltpu.VMEM((nface, up(nbox, 128)), bf16),
        pltpu.VMEM((3 * kp, nq * e), bf16),
        pltpu.VMEM((3 * nb + 4 * jp, nq * e), f32),
        pltpu.VMEM((nq, nb, e), f32),
        pltpu.VMEM((nq, nb, e), f32),
        pltpu.VMEM((nq, nb, e), f32),
        pltpu.VMEM((mrow, nface), f32),
        pltpu.VMEM((mrow, nface), f32),
        pltpu.VMEM((4 * jp, nq * e), f32),
        pltpu.VMEM((4 * jp, nq * e), f32),
        pltpu.VMEM((TICKS, nbox, prow), f32),
        pltpu.VMEM((TICKS, nbox, prow), f32),
        pltpu.SemaphoreType.DMA((TICKS, 6)),
        pltpu.SemaphoreType.DMA((TICKS, 6)),
    ]
    operands = (
        jnp.transpose(state, (1, 0, 2)), stiffness, volume_matrix,
        jnp.transpose(trace_matrix, (1, 0, 2)), jnp.transpose(lift_matrix, (2, 0, 1)), rotation,
        *(jnp.transpose(m, (1, 2, 0, 3)) for m in (star_matrix, flux_minus, flux_plus)),
        face_orient, face_source, boundary_face,
    )
    held = [pltpu.VMEM(x.shape, x.dtype) for x in operands[1:]]
    out = pl.pallas_call(
        functools.partial(kernel, (nb, nq, nf, e, slots)),
        out_shape=jax.ShapeDtypeStruct((nq, nb, e), f32),
        in_specs=[pl.BlockSpec(memory_space=pltpu.SMEM)] + [pl.BlockSpec(memory_space=pltpu.HBM)] * 12,
        out_specs=vmem,
        scratch_shapes=held + scratch,
        compiler_params=pltpu.CompilerParams(
            collective_id=0, has_side_effects=True, vmem_limit_bytes=67043328
        ),
    )(patch_rate, *operands)
    return jnp.transpose(out, (1, 0, 2))


def solution(mesh):
    both = ("dom", "region")
    return jax.shard_map(
        local,
        mesh=mesh,
        in_specs=(
            P(None, None, both), P(), P(), P(), P(), P(),
            P(None, None, None, both), P(None, None, None, both), P(None, None, None, both),
            P(both), P(None, both), P(None, both), P(None, both),
        ),
        out_specs=P(None, None, both),
        check_vma=False,
    )
```

```python
import functools
import math

import jax
import jax.numpy as jnp
from jax import lax
from jax.experimental import pallas as pl
from jax.experimental.pallas import tpu as pltpu
from jax.sharding import PartitionSpec as P

MESH = pl.DeviceIdType.MESH
TERMS = 6
TICKS = 4
PATCH = 128
STEP_LENGTH = 1.5
f32 = jnp.float32
bf16 = jnp.bfloat16

MOVES = (("dom", 1), ("dom", -1), ("dom", 2), ("dom", -2), ("region", 1), ("region", -1))


def up(n, m):
    return -(-n // m) * m


def high_part(x):
    return x.astype(bf16).astype(f32)


def dot(a, b):
    return jnp.dot(a, b, preferred_element_type=f32)


def kernel(
    sizes,
    rate_ref, *refs,
):
    sources, out_ref, held = refs[:12], refs[12], refs[13:24]
    (
        coef, load_sem, wk, wv, wt, wl, wr, tmp, pick_in, pick_out,
        xs, y, itick, terms, volume, pool, acc, own, flux, send_buf, recv_buf,
        send_sem, recv_sem,
    ) = refs[24:]
    (
        stiff_ref, vol_ref, trace_ref, lift_ref, rot_ref,
        star_ref, minus_ref, plus_ref, orient_ref, source_ref, bound_ref,
    ) = held
    loads = [
        pltpu.make_async_copy(src, dst, load_sem.at[i])
        for i, (src, dst) in enumerate(zip(sources, (out_ref, *held)))
    ]
    for i in (1, 2, 3, 4, 5, 10, 11, 0, 6, 7, 8, 9):
        loads[i].start()
    nb, nq, nf, e, slots = sizes
    kp = up(nb, 16)
    jp = up(nf, 8)
    rows = nq * jp
    prow = send_buf.shape[2]
    mrow = pool.shape[0]
    nface = 4 * e
    nbox = 6 * slots
    place = {"dom": lax.axis_index("dom"), "region": lax.axis_index("region")}
    extent = {"dom": lax.axis_size("dom"), "region": lax.axis_size("region")}
    there = []
    for axis, offset in MOVES:
        target = place[axis] + offset
        there.append((target >= 0) & (target < extent[axis]))

    recv_buf[...] = jnp.zeros_like(recv_buf)

    barrier = pltpu.get_barrier_semaphore()
    count = jnp.int32(0)
    for (axis, offset), ok in zip(MOVES, there):
        @pl.when(ok)
        def _():
            pl.semaphore_signal(barrier, inc=1, device_id={axis: place[axis] + offset}, device_id_type=MESH)
        count = count + ok.astype(jnp.int32)

    for i in (1, 2, 3, 4, 5):
        loads[i].wait()

    def left(dst, blocks, stride, width):
        tmp[...] = jnp.zeros_like(tmp)
        for row, lane, value in blocks:
            hi = high_part(value)
            lo = value - hi
            r, c = value.shape
            for i, part in enumerate((hi, hi, lo)):
                tmp[row:row + r, i * stride + lane:i * stride + lane + c] = part
        dst[...] = tmp[0:dst.shape[0], 0:dst.shape[1]].astype(bf16)

    left(wk, [(d * nb, 0, -stiff_ref[d]) for d in range(3)], kp, nb)
    left(wv, [(d * nb, 0, vol_ref[d]) for d in range(3)]
         + [(3 * nb + f * jp, 0, trace_ref[:, f, :]) for f in range(4)], kp, nb)
    left(wt, [(f * jp, 0, trace_ref[:, f, :]) for f in range(4)], kp, nb)
    left(wl, [(0, f * jp, -jnp.transpose(lift_ref[:, f, :])) for f in range(4)], 4 * jp, nf)
    left(wr, [(o * jp, 0, rot_ref[o]) for o in range(3)], jp, nf)

    loads[10].wait()
    loads[11].wait()

    for f in range(4):
        want = source_ref[f:f + 1, :]
        ids = lax.broadcasted_iota(jnp.int32, (pick_in.shape[0], e), 0)
        pick_in[:, f * e:(f + 1) * e] = (ids == want).astype(f32).astype(bf16)
    ids = lax.broadcasted_iota(jnp.int32, (nface, slots), 0)
    tmp[...] = jnp.zeros_like(tmp)
    for k in range(6):
        tmp[0:nface, k * slots:(k + 1) * slots] = (ids == bound_ref[k:k + 1, :]).astype(f32)
    pick_out[...] = tmp[0:nface, 0:pick_out.shape[1]].astype(bf16)

    xs[...] = jnp.zeros_like(xs)
    pool[...] = jnp.zeros_like(pool)
    acc[...] = jnp.zeros_like(acc)
    for i in (0, 6, 7, 8, 9):
        loads[i].wait()

    rate = rate_ref[0]
    span = jnp.where(rate == 1, 4, jnp.where(rate == 2, 2, 1))
    width = STEP_LENGTH / TICKS
    step_width = span.astype(f32) * width

    pl.semaphore_wait(barrier, count)

    def cols(q):
        if isinstance(q, int):
            return slice(q * e, (q + 1) * e)
        return pl.ds(pl.multiple_of(q * e, e), e)

    def put(q, value):
        pad = jnp.zeros((kp - nb, e), f32)
        hi = high_part(value)
        lo = value - hi
        hib = jnp.concatenate([hi, pad], axis=0).astype(bf16)
        xs[0:kp, cols(q)] = hib
        xs[kp:2 * kp, cols(q)] = jnp.concatenate([lo, pad], axis=0).astype(bf16)
        xs[2 * kp:3 * kp, cols(q)] = hib

    def starred(group):
        sums = [None] * len(group)
        for d in range(3):
            for q in range(nq):
                term = y[d * nb:(d + 1) * nb, cols(q)]
                for i, p in enumerate(group):
                    part = star_ref[p, q, d:d + 1, :] * term
                    sums[i] = part if sums[i] is None else sums[i] + part
        return sums

    gsize = next(n for n in (3, 2, 1) if nq % n == 0)

    def by_group(use):
        def body(g, c):
            use([g * gsize + i for i in range(gsize)])
            return c

        lax.fori_loop(0, nq // gsize, body, 0)

    def both(value):
        hi = high_part(value)
        return jnp.concatenate([hi, value - hi], axis=0).astype(bf16)

    def gather(value, table):
        n = value.shape[0]
        result = dot(both(value), table)
        return result[0:n] + result[n:2 * n]

    def solver(matrix_ref, group, start, field, base):
        for f in range(4):
            sums = [start(f, p) for p in group]
            for q in range(nq):
                term = field[base + f * jp:base + (f + 1) * jp, cols(q)]
                for i, p in enumerate(group):
                    part = matrix_ref[p, q, f:f + 1, :] * term
                    sums[i] = part if sums[i] is None else sums[i] + part
            for p, value in zip(group, sums):
                own[f * jp:(f + 1) * jp, cols(p)] = value

    def tick(t, carry):
        offset = lax.bitwise_and(t, span - 1)
        lower = offset.astype(f32) * width
        upper = lower + width
        lo_pow, up_pow, st_pow = lower, upper, step_width
        for k in range(TERMS):
            factor = 1.0 / math.factorial(k + 1)
            coef[0, k] = (up_pow - lo_pow) * factor
            coef[1, k] = st_pow * factor
            lo_pow, up_pow, st_pow = lo_pow * lower, up_pow * upper, st_pow * step_width
        keep = jnp.where(offset == 0, 0.0, 1.0).astype(f32)
        finish = jnp.where(offset == span - 1, 1.0, 0.0).astype(f32)

        for q in range(nq):
            value = out_ref[q]
            itick[q] = coef[0, 0] * value
            put(q, value)

        def degree(k, c):
            y[0:3 * nb, :] = dot(wk[...], xs[...])
            ct = coef[0, k]

            def use(group):
                for p, value in zip(group, starred(group)):
                    itick[p] = itick[p] + ct * value
                    terms[k, p] = value
                    put(p, value)

            by_group(use)
            return c

        lax.fori_loop(1, TERMS, degree, 0)

        for q in range(nq):
            put(q, itick[q])
        traces = dot(wt[...], xs[...])
        for q in range(nq):
            for f in range(4):
                pool[q * jp:(q + 1) * jp, f * e:(f + 1) * e] = traces[f * jp:(f + 1) * jp, cols(q)]
        pooled = pool[0:mrow, :]
        picked = gather(pooled, pick_out[...])
        if prow > mrow:
            picked = jnp.concatenate([picked, jnp.zeros((prow - mrow, picked.shape[1]), f32)], axis=0)
        send_buf[t] = jnp.transpose(picked)[0:nbox]

        def box(k):
            axis, step = MOVES[k]
            return pltpu.make_async_remote_copy(
                src_ref=send_buf.at[t, pl.ds(k * slots, slots)],
                dst_ref=recv_buf.at[t, pl.ds((k ^ 1) * slots, slots)],
                send_sem=send_sem.at[t, k],
                recv_sem=recv_sem.at[t, k ^ 1],
                device_id={axis: place[axis] + step},
                device_id_type=MESH,
            )

        for k in (2, 3, 0, 1, 4, 5):
            @pl.when(there[k])
            def _():
                box(k).start()

        acc[...] = acc[...] * keep + gather(pooled, pick_in[0:nface, :])
        for q in range(nq):
            value = coef[1, 0] * out_ref[q]
            for k in range(1, TERMS):
                value = value + coef[1, k] * terms[k, q]
            put(q, value)
        y[...] = dot(wv[...], xs[...])

        def use(group):
            for p, value in zip(group, starred(group)):
                volume[p] = value
            solver(minus_ref, group, lambda f, p: None, y, 3 * nb)

        by_group(use)

        for k in range(6):
            @pl.when(there[k])
            def _():
                axis, step = MOVES[k]
                pltpu.make_async_remote_copy(
                    src_ref=send_buf.at[t, pl.ds(k * slots, slots)],
                    dst_ref=recv_buf.at[t, pl.ds(k * slots, slots)],
                    send_sem=send_sem.at[t, k],
                    recv_sem=recv_sem.at[t, k],
                    device_id={axis: place[axis] + step},
                    device_id_type=MESH,
                ).wait()

        came = jnp.transpose(recv_buf[t])[0:mrow]
        acc[...] = acc[...] + gather(came, pick_in[nface:nface + nbox, :])

        spare = jnp.zeros((wr.shape[1] - 3 * jp, nface), f32)
        for q in range(nq):
            value = acc[q * jp:(q + 1) * jp, :]
            hi = high_part(value)
            stack = jnp.concatenate([hi, value - hi, hi, spare], axis=0).astype(bf16)
            y[0:3 * jp, 0:nface] = dot(wr[...], stack)
            for f in range(4):
                orient = orient_ref[f:f + 1, :]
                r0 = y[0:jp, f * e:(f + 1) * e]
                r1 = y[jp:2 * jp, f * e:(f + 1) * e]
                r2 = y[2 * jp:3 * jp, f * e:(f + 1) * e]
                flux[f * jp:(f + 1) * jp, cols(q)] = jnp.where(orient == 0, r0, jnp.where(orient == 1, r1, r2))
        by_group(lambda group: solver(plus_ref, group, lambda f, p: own[f * jp:(f + 1) * jp, cols(p)], flux, 0))
        value = own[...]
        hi = high_part(value)
        stack = jnp.concatenate([hi, value - hi, hi], axis=0).astype(bf16)
        y[0:nb, :] = dot(wl[...], stack)
        for p in range(nq):
            now = out_ref[p]
            out_ref[p] = jnp.where(finish > 0.5, now + (volume[p] + y[0:nb, cols(p)]), now)
        return carry

    lax.fori_loop(0, TICKS, tick, 0)


def local(
    state, stiffness, volume_matrix, trace_matrix, lift_matrix, rotation, star_matrix,
    flux_minus, flux_plus, patch_rate, face_orient, face_source, boundary_face,
):
    nb, nq, e = state.shape
    nf = rotation.shape[1]
    slots = boundary_face.shape[1]
    assert patch_rate.shape[0] * PATCH == e and patch_rate.shape[0] == 1
    kp, jp = up(nb, 16), up(nf, 8)
    nface, nbox = 4 * e, 6 * slots
    mrow = up(nq * jp, 16)
    prow = up(mrow, 128)
    vmem = pl.BlockSpec(memory_space=pltpu.VMEM)
    scratch = [
        pltpu.SMEM((2, 8), f32),
        pltpu.SemaphoreType.DMA((12,)),
        pltpu.VMEM((3 * nb, 3 * kp), bf16),
        pltpu.VMEM((3 * nb + 4 * jp, 3 * kp), bf16),
        pltpu.VMEM((4 * jp, 3 * kp), bf16),
        pltpu.VMEM((nb, 12 * jp), bf16),
        pltpu.VMEM((3 * jp, up(3 * jp, 16)), bf16),
        pltpu.VMEM((nface, 3 * 128), f32),
        pltpu.VMEM((nface + nbox, nface), bf16),
        pltpu.VMEM((nface, up(nbox, 128)), bf16),
        pltpu.VMEM((3 * kp, nq * e), bf16),
        pltpu.VMEM((3 * nb + 4 * jp, nq * e), f32),
        pltpu.VMEM((nq, nb, e), f32),
        pltpu.VMEM((TERMS, nq, nb, e), f32),
        pltpu.VMEM((nq, nb, e), f32),
        pltpu.VMEM((mrow, nface), f32),
        pltpu.VMEM((mrow, nface), f32),
        pltpu.VMEM((4 * jp, nq * e), f32),
        pltpu.VMEM((4 * jp, nq * e), f32),
        pltpu.VMEM((TICKS, nbox, prow), f32),
        pltpu.VMEM((TICKS, nbox, prow), f32),
        pltpu.SemaphoreType.DMA((TICKS, 6)),
        pltpu.SemaphoreType.DMA((TICKS, 6)),
    ]
    operands = (
        jnp.transpose(state, (1, 0, 2)), stiffness, volume_matrix,
        jnp.transpose(trace_matrix, (1, 0, 2)), jnp.transpose(lift_matrix, (2, 0, 1)), rotation,
        *(jnp.transpose(m, (1, 2, 0, 3)) for m in (star_matrix, flux_minus, flux_plus)),
        face_orient, face_source, boundary_face,
    )
    held = [pltpu.VMEM(x.shape, x.dtype) for x in operands[1:]]
    out = pl.pallas_call(
        functools.partial(kernel, (nb, nq, nf, e, slots)),
        out_shape=jax.ShapeDtypeStruct((nq, nb, e), f32),
        in_specs=[pl.BlockSpec(memory_space=pltpu.SMEM)] + [pl.BlockSpec(memory_space=pltpu.HBM)] * 12,
        out_specs=vmem,
        scratch_shapes=held + scratch,
        compiler_params=pltpu.CompilerParams(
            collective_id=0, has_side_effects=True, vmem_limit_bytes=67043328
        ),
    )(patch_rate, *operands)
    return jnp.transpose(out, (1, 0, 2))


def solution(mesh):
    both = ("dom", "region")
    return jax.shard_map(
        local,
        mesh=mesh,
        in_specs=(
            P(None, None, both), P(), P(), P(), P(), P(),
            P(None, None, None, both), P(None, None, None, both), P(None, None, None, both),
            P(both), P(None, both), P(None, both), P(None, both),
        ),
        out_specs=P(None, None, both),
        check_vma=False,
    )
```

```python
import functools
import math

import jax
import jax.numpy as jnp
from jax import lax
from jax.experimental import pallas as pl
from jax.experimental.pallas import tpu as pltpu
from jax.sharding import PartitionSpec as P

MESH = pl.DeviceIdType.MESH
TERMS = 6
TICKS = 4
PATCH = 128
STEP_LENGTH = 1.5
f32 = jnp.float32
bf16 = jnp.bfloat16

MOVES = (("dom", 1), ("dom", -1), ("dom", 2), ("dom", -2), ("region", 1), ("region", -1))


def up(n, m):
    return -(-n // m) * m


def high_part(x):
    return x.astype(bf16).astype(f32)


def dot(a, b):
    return jnp.dot(a, b, preferred_element_type=f32)


def kernel(
    sizes,
    rate_ref, *refs,
):
    sources, out_ref, held = refs[:12], refs[12], refs[13:24]
    (
        coef, load_sem, wk, wv, wt, wl, wr, tmp, pick_in, pick_out,
        xs, y, itick, terms, volume, pool, acc, own, flux, send_buf, recv_buf,
        send_sem, recv_sem,
    ) = refs[24:]
    (
        stiff_ref, vol_ref, trace_ref, lift_ref, rot_ref,
        star_ref, minus_ref, plus_ref, orient_ref, source_ref, bound_ref,
    ) = held
    loads = [
        pltpu.make_async_copy(src, dst, load_sem.at[i])
        for i, (src, dst) in enumerate(zip(sources, (out_ref, *held)))
    ]
    for i in (1, 2, 3, 4, 5, 10, 11, 0, 6, 7, 8, 9):
        loads[i].start()
    nb, nq, nf, e, slots = sizes
    kp = up(nb, 16)
    jp = up(nf, 8)
    rows = nq * jp
    prow = send_buf.shape[2]
    mrow = pool.shape[0]
    nface = 4 * e
    nbox = 6 * slots
    place = {"dom": lax.axis_index("dom"), "region": lax.axis_index("region")}
    extent = {"dom": lax.axis_size("dom"), "region": lax.axis_size("region")}
    there = []
    for axis, offset in MOVES:
        target = place[axis] + offset
        there.append((target >= 0) & (target < extent[axis]))

    recv_buf[...] = jnp.zeros_like(recv_buf)

    barrier = pltpu.get_barrier_semaphore()
    count = jnp.int32(0)
    for (axis, offset), ok in zip(MOVES, there):
        @pl.when(ok)
        def _():
            pl.semaphore_signal(barrier, inc=1, device_id={axis: place[axis] + offset}, device_id_type=MESH)
        count = count + ok.astype(jnp.int32)

    for i in (1, 2, 3, 4, 5):
        loads[i].wait()

    def left(dst, blocks, stride, width):
        tmp[...] = jnp.zeros_like(tmp)
        for row, lane, value in blocks:
            hi = high_part(value)
            lo = value - hi
            r, c = value.shape
            for i, part in enumerate((hi, hi, lo)):
                tmp[row:row + r, i * stride + lane:i * stride + lane + c] = part
        dst[...] = tmp[0:dst.shape[0], 0:dst.shape[1]].astype(bf16)

    left(wk, [(d * nb, 0, -stiff_ref[d]) for d in range(3)], kp, nb)
    left(wv, [(d * nb, 0, vol_ref[d]) for d in range(3)]
         + [(3 * nb + f * jp, 0, trace_ref[:, f, :]) for f in range(4)], kp, nb)
    left(wt, [(f * jp, 0, trace_ref[:, f, :]) for f in range(4)], kp, nb)
    left(wl, [(0, f * jp, -jnp.transpose(lift_ref[:, f, :])) for f in range(4)], 4 * jp, nf)
    left(wr, [(o * jp, 0, rot_ref[o]) for o in range(3)], jp, nf)

    loads[10].wait()
    loads[11].wait()

    for f in range(4):
        want = source_ref[f:f + 1, :]
        ids = lax.broadcasted_iota(jnp.int32, (pick_in.shape[0], e), 0)
        pick_in[:, f * e:(f + 1) * e] = (ids == want).astype(f32).astype(bf16)
    ids = lax.broadcasted_iota(jnp.int32, (nface, slots), 0)
    tmp[...] = jnp.zeros_like(tmp)
    for k in range(6):
        tmp[0:nface, k * slots:(k + 1) * slots] = (ids == bound_ref[k:k + 1, :]).astype(f32)
    pick_out[...] = tmp[0:nface, 0:pick_out.shape[1]].astype(bf16)

    xs[...] = jnp.zeros_like(xs)
    pool[...] = jnp.zeros_like(pool)
    acc[...] = jnp.zeros_like(acc)
    for i in (0, 6, 7, 8, 9):
        loads[i].wait()

    rate = rate_ref[0]
    span = jnp.where(rate == 1, 4, jnp.where(rate == 2, 2, 1))
    width = STEP_LENGTH / TICKS
    step_width = span.astype(f32) * width

    pl.semaphore_wait(barrier, count)

    def cols(q):
        if isinstance(q, int):
            return slice(q * e, (q + 1) * e)
        return pl.ds(pl.multiple_of(q * e, e), e)

    def put(q, value):
        pad = jnp.zeros((kp - nb, e), f32)
        hi = high_part(value)
        lo = value - hi
        hib = jnp.concatenate([hi, pad], axis=0).astype(bf16)
        xs[0:kp, cols(q)] = hib
        xs[kp:2 * kp, cols(q)] = jnp.concatenate([lo, pad], axis=0).astype(bf16)
        xs[2 * kp:3 * kp, cols(q)] = hib

    def starred(group):
        sums = [None] * len(group)
        for d in range(3):
            for q in range(nq):
                term = y[d * nb:(d + 1) * nb, cols(q)]
                for i, p in enumerate(group):
                    part = star_ref[p, q, d:d + 1, :] * term
                    sums[i] = part if sums[i] is None else sums[i] + part
        return sums

    gsize = next(n for n in (3, 2, 1) if nq % n == 0)

    def by_group(use):
        def body(g, c):
            use([g * gsize + i for i in range(gsize)])
            return c

        lax.fori_loop(0, nq // gsize, body, 0)

    def both(value):
        hi = high_part(value)
        return jnp.concatenate([hi, value - hi], axis=0).astype(bf16)

    def gather(value, table):
        n = value.shape[0]
        result = dot(both(value), table)
        return result[0:n] + result[n:2 * n]

    def solver(matrix_ref, group, start, field, base):
        for f in range(4):
            sums = [start(f, p) for p in group]
            for q in range(nq):
                term = field[base + f * jp:base + (f + 1) * jp, cols(q)]
                for i, p in enumerate(group):
                    part = matrix_ref[p, q, f:f + 1, :] * term
                    sums[i] = part if sums[i] is None else sums[i] + part
            for p, value in zip(group, sums):
                own[f * jp:(f + 1) * jp, cols(p)] = value

    def tick(t, carry):
        offset = lax.bitwise_and(t, span - 1)
        lower = offset.astype(f32) * width
        upper = lower + width
        lo_pow, up_pow, st_pow = lower, upper, step_width
        for k in range(TERMS):
            factor = 1.0 / math.factorial(k + 1)
            coef[0, k] = (up_pow - lo_pow) * factor
            coef[1, k] = st_pow * factor
            lo_pow, up_pow, st_pow = lo_pow * lower, up_pow * upper, st_pow * step_width
        keep = jnp.where(offset == 0, 0.0, 1.0).astype(f32)
        finish = jnp.where(offset == span - 1, 1.0, 0.0).astype(f32)

        for q in range(nq):
            value = out_ref[q]
            itick[q] = coef[0, 0] * value
            put(q, value)

        def degree(k, c, last=False):
            y[0:3 * nb, :] = dot(wk[...], xs[...])
            ct = coef[0, k]

            def use(group):
                for p, value in zip(group, starred(group)):
                    total = itick[p] + ct * value
                    itick[p] = total
                    terms[k, p] = value
                    put(p, total if last else value)

            by_group(use)
            return c

        lax.fori_loop(1, TERMS - 1, degree, 0)
        degree(TERMS - 1, 0, last=True)

        traces = dot(wt[...], xs[...])
        for q in range(nq):
            for f in range(4):
                pool[q * jp:(q + 1) * jp, f * e:(f + 1) * e] = traces[f * jp:(f + 1) * jp, cols(q)]
        pooled = pool[0:mrow, :]
        picked = gather(pooled, pick_out[...])
        if prow > mrow:
            picked = jnp.concatenate([picked, jnp.zeros((prow - mrow, picked.shape[1]), f32)], axis=0)
        send_buf[t] = jnp.transpose(picked)[0:nbox]

        def box(k):
            axis, step = MOVES[k]
            return pltpu.make_async_remote_copy(
                src_ref=send_buf.at[t, pl.ds(k * slots, slots)],
                dst_ref=recv_buf.at[t, pl.ds((k ^ 1) * slots, slots)],
                send_sem=send_sem.at[t, k],
                recv_sem=recv_sem.at[t, k ^ 1],
                device_id={axis: place[axis] + step},
                device_id_type=MESH,
            )

        for k in (2, 3, 0, 1, 4, 5):
            @pl.when(there[k])
            def _():
                box(k).start()

        acc[...] = acc[...] * keep + gather(pooled, pick_in[0:nface, :])
        for q in range(nq):
            value = coef[1, 0] * out_ref[q]
            for k in range(1, TERMS):
                value = value + coef[1, k] * terms[k, q]
            put(q, value)
        y[...] = dot(wv[...], xs[...])

        def use(group):
            for p, value in zip(group, starred(group)):
                volume[p] = value
            solver(minus_ref, group, lambda f, p: None, y, 3 * nb)

        by_group(use)

        for k in range(6):
            @pl.when(there[k])
            def _():
                axis, step = MOVES[k]
                pltpu.make_async_remote_copy(
                    src_ref=send_buf.at[t, pl.ds(k * slots, slots)],
                    dst_ref=recv_buf.at[t, pl.ds(k * slots, slots)],
                    send_sem=send_sem.at[t, k],
                    recv_sem=recv_sem.at[t, k],
                    device_id={axis: place[axis] + step},
                    device_id_type=MESH,
                ).wait()

        came = jnp.transpose(recv_buf[t])[0:mrow]
        acc[...] = acc[...] + gather(came, pick_in[nface:nface + nbox, :])

        spare = jnp.zeros((wr.shape[1] - 3 * jp, nface), f32)
        for q in range(nq):
            value = acc[q * jp:(q + 1) * jp, :]
            hi = high_part(value)
            stack = jnp.concatenate([hi, value - hi, hi, spare], axis=0).astype(bf16)
            y[0:3 * jp, 0:nface] = dot(wr[...], stack)
            for f in range(4):
                orient = orient_ref[f:f + 1, :]
                r0 = y[0:jp, f * e:(f + 1) * e]
                r1 = y[jp:2 * jp, f * e:(f + 1) * e]
                r2 = y[2 * jp:3 * jp, f * e:(f + 1) * e]
                flux[f * jp:(f + 1) * jp, cols(q)] = jnp.where(orient == 0, r0, jnp.where(orient == 1, r1, r2))
        by_group(lambda group: solver(plus_ref, group, lambda f, p: own[f * jp:(f + 1) * jp, cols(p)], flux, 0))
        value = own[...]
        hi = high_part(value)
        stack = jnp.concatenate([hi, value - hi, hi], axis=0).astype(bf16)
        y[0:nb, :] = dot(wl[...], stack)
        for p in range(nq):
            now = out_ref[p]
            out_ref[p] = jnp.where(finish > 0.5, now + (volume[p] + y[0:nb, cols(p)]), now)
        return carry

    lax.fori_loop(0, TICKS, tick, 0)


def local(
    state, stiffness, volume_matrix, trace_matrix, lift_matrix, rotation, star_matrix,
    flux_minus, flux_plus, patch_rate, face_orient, face_source, boundary_face,
):
    nb, nq, e = state.shape
    nf = rotation.shape[1]
    slots = boundary_face.shape[1]
    assert patch_rate.shape[0] * PATCH == e and patch_rate.shape[0] == 1
    kp, jp = up(nb, 16), up(nf, 8)
    nface, nbox = 4 * e, 6 * slots
    mrow = up(nq * jp, 16)
    prow = up(mrow, 128)
    vmem = pl.BlockSpec(memory_space=pltpu.VMEM)
    scratch = [
        pltpu.SMEM((2, 8), f32),
        pltpu.SemaphoreType.DMA((12,)),
        pltpu.VMEM((3 * nb, 3 * kp), bf16),
        pltpu.VMEM((3 * nb + 4 * jp, 3 * kp), bf16),
        pltpu.VMEM((4 * jp, 3 * kp), bf16),
        pltpu.VMEM((nb, 12 * jp), bf16),
        pltpu.VMEM((3 * jp, up(3 * jp, 16)), bf16),
        pltpu.VMEM((nface, 3 * 128), f32),
        pltpu.VMEM((nface + nbox, nface), bf16),
        pltpu.VMEM((nface, up(nbox, 128)), bf16),
        pltpu.VMEM((3 * kp, nq * e), bf16),
        pltpu.VMEM((3 * nb + 4 * jp, nq * e), f32),
        pltpu.VMEM((nq, nb, e), f32),
        pltpu.VMEM((TERMS, nq, nb, e), f32),
        pltpu.VMEM((nq, nb, e), f32),
        pltpu.VMEM((mrow, nface), f32),
        pltpu.VMEM((mrow, nface), f32),
        pltpu.VMEM((4 * jp, nq * e), f32),
        pltpu.VMEM((4 * jp, nq * e), f32),
        pltpu.VMEM((TICKS, nbox, prow), f32),
        pltpu.VMEM((TICKS, nbox, prow), f32),
        pltpu.SemaphoreType.DMA((TICKS, 6)),
        pltpu.SemaphoreType.DMA((TICKS, 6)),
    ]
    operands = (
        jnp.transpose(state, (1, 0, 2)), stiffness, volume_matrix,
        jnp.transpose(trace_matrix, (1, 0, 2)), jnp.transpose(lift_matrix, (2, 0, 1)), rotation,
        *(jnp.transpose(m, (1, 2, 0, 3)) for m in (star_matrix, flux_minus, flux_plus)),
        face_orient, face_source, boundary_face,
    )
    held = [pltpu.VMEM(x.shape, x.dtype) for x in operands[1:]]
    out = pl.pallas_call(
        functools.partial(kernel, (nb, nq, nf, e, slots)),
        out_shape=jax.ShapeDtypeStruct((nq, nb, e), f32),
        in_specs=[pl.BlockSpec(memory_space=pltpu.SMEM)] + [pl.BlockSpec(memory_space=pltpu.HBM)] * 12,
        out_specs=vmem,
        scratch_shapes=held + scratch,
        compiler_params=pltpu.CompilerParams(
            collective_id=0, has_side_effects=True, vmem_limit_bytes=67043328
        ),
    )(patch_rate, *operands)
    return jnp.transpose(out, (1, 0, 2))


def solution(mesh):
    both = ("dom", "region")
    return jax.shard_map(
        local,
        mesh=mesh,
        in_specs=(
            P(None, None, both), P(), P(), P(), P(), P(),
            P(None, None, None, both), P(None, None, None, both), P(None, None, None, both),
            P(both), P(None, both), P(None, both), P(None, both),
        ),
        out_specs=P(None, None, both),
        check_vma=False,
    )
```
